128 devices in a mesh: tm: 8 (over y_hi, z), height: 4 (over x), head: 4 (over y_lo, core).
Axes of the slice: x: 4, y: 4 (y_hi: 2, y_lo: 2; y = y_hi * 2 + y_lo), z: 4, core: 2. Of those that a mesh axis runs over, the one named last changes fastest.
Arguments:
- query_in: bfloat16 [12, 32, 32, 16, 128], P('head', 'tm', 'height'), may hold values from -8 to 8
- key_in: bfloat16 [12, 32, 32, 16, 128], P('head', 'tm', 'height'), may hold values from -8 to 8
- value_in: bfloat16 [12, 32, 32, 16, 128], P('head', 'tm', 'height'), may hold values from -6 to 6
- out_grad: bfloat16 [12, 32, 32, 16, 128], P('head', 'tm', 'height'), may hold values from -6 to 6
Outputs:
- query_grad: bfloat16 [12, 32, 32, 16, 128], P('head', 'tm', 'height')
- key_grad: bfloat16 [12, 32, 32, 16, 128], P('head', 'tm', 'height')
- value_grad: bfloat16 [12, 32, 32, 16, 128], P('head', 'tm', 'height')
The draws below stay inside these ranges and needn't reach their ends.
All inputs are finite; a program needn't handle non-finite values.
Results may differ from the reference program's by a relative error of at most 0.0093.
Values may be sent and summed in bfloat16 or wider, within the bound.
No kernel may reach another device: no remote copies, remote signals or barrier semaphores. Data moves between devices by JAX's collectives and lax.ppermute only.
A program may use at most 128 MiB of HBM per device.

```python
import jax
import jax.numpy as jnp
from jax import lax

HEADS = 12
HEAD_DIM = 128
TILE_F = 4
TILE_R = 8
TILE_C = 8
COLS = 16
NF = 32
NR = 32


def draw_pair(key):
    full_shape = (HEADS, NF, NR, COLS, HEAD_DIM)
    seed_list = jax.random.split(jax.random.fold_in(key, 41), 2)
    query_draw = jax.random.truncated_normal(seed_list[0], -4.0, 4.0, full_shape, jnp.float32)
    key_draw = jax.random.truncated_normal(seed_list[1], -4.0, 4.0, full_shape, jnp.float32)
    return (query_draw, key_draw)


def draw_query_in(key, part):
    return draw_pair(key)[0].astype(jnp.bfloat16)


def draw_key_in(key, part):
    return draw_pair(key)[1].astype(jnp.bfloat16)


def levels(rng, shape, pieces, least, high):
    def one(axis_at, blocks):
        draws = jax.random.uniform(jax.random.fold_in(jax.random.fold_in(rng, 6), axis_at), (blocks,), jnp.float32, least / len(pieces), high / len(pieces))
        return jnp.repeat(jnp.exp(draws), shape[axis_at] // blocks).reshape((-1,) + (1,) * (len(shape) - axis_at - 1))

    factor_of = one(*pieces[0])
    for cut in pieces[1:]:
        factor_of = factor_of * one(*cut)
    return factor_of


def centred(own_key, shape, scale, reach, pieces=(), held_as=jnp.bfloat16):
    level = levels(own_key, shape, pieces, -0.22, 0.18) if pieces else 1.0
    array = jax.random.normal(own_key, shape, jnp.float32) * scale * level
    return jnp.minimum(jnp.maximum(array, -reach), reach).astype(held_as)


def setup_inputs(seed: int = 0) -> dict:
    keys = jax.random.split(jax.random.key(seed), 5)
    return {
        "query_in": draw_query_in(jax.random.fold_in(keys[4], 71), 0),
        "key_in": draw_key_in(jax.random.fold_in(keys[4], 71), 0),
        "value_in": centred(keys[2], (HEADS, NF, NR, COLS, HEAD_DIM), 1.0, 6.0, ((0, 4), (1, 8), (2, 4))),
        "out_grad": centred(keys[3], (HEADS, NF, NR, COLS, HEAD_DIM), 1.0, 6.0, ((0, 4), (1, 8), (2, 4))),
    }


def rounded(values):
    return lax.optimization_barrier(values.astype(jnp.bfloat16)).astype(jnp.float32)


def batched(form, left_op, right_op):
    return jnp.einsum(form, left_op.astype(jnp.float32), right_op.astype(jnp.float32))


def corner_at(first, second, third, rank):
    anchor = jnp.zeros((), jnp.int32)
    middle = (first.astype(jnp.int32), second.astype(jnp.int32), third.astype(jnp.int32))
    return (anchor,) + middle + (anchor,) * (rank - 4)


def tiles_back(stacked, grid_f, grid_r, grid_c):
    head_count, tile_f, tile_r, tile_c = stacked.shape[1:5]
    trailing = stacked.shape[5:]
    split = stacked.reshape((grid_f, grid_r, grid_c, head_count, tile_f, tile_r, tile_c) + trailing)
    order = (3, 0, 4, 1, 5, 2, 6) + tuple(range(7, 7 + len(trailing)))
    return split.transpose(order).reshape((head_count, grid_f * tile_f, grid_r * tile_r, grid_c * tile_c) + trailing)


def reference(query_in, key_in, value_in, out_grad):
    head_count, frame_count, row_count, col_count, head_depth = query_in.shape
    score_scale = head_depth ** -0.5
    grid_f = frame_count // TILE_F
    grid_r = row_count // TILE_R
    grid_c = col_count // TILE_C
    border = ((0, 0), (TILE_F, TILE_F), (TILE_R, TILE_R), (TILE_C, TILE_C), (0, 0))
    inside = jnp.pad(jnp.ones((1, frame_count, row_count, col_count, 1), jnp.float32), border)
    tile_shape = (head_count, TILE_F, TILE_R, TILE_C, head_depth)
    span_shape = (head_count, 3 * TILE_F, 3 * TILE_R, 3 * TILE_C, head_depth)
    mask_shape = (1, 3 * TILE_F, 3 * TILE_R, 3 * TILE_C, 1)
    stat_tile = tile_shape[:4]
    stat_span = span_shape[:4]
    key_pad = jnp.pad(key_in, border)
    value_pad = jnp.pad(value_in, border)

    def tile_place(tile_index):
        first = tile_index // (grid_r * grid_c)
        second = (tile_index // grid_c) % grid_r
        third = tile_index % grid_c
        return first * TILE_F, second * TILE_R, third * TILE_C

    def query_tile(tile_index):
        first, second, third = tile_place(tile_index)
        corner = corner_at(first, second, third, 5)
        q_rows = lax.dynamic_slice(query_in, corner, tile_shape).reshape(head_count, -1, head_depth)
        g_rows = lax.dynamic_slice(out_grad, corner, tile_shape).reshape(head_count, -1, head_depth)
        k_span = lax.dynamic_slice(key_pad, corner, span_shape).reshape(head_count, -1, head_depth)
        v_span = lax.dynamic_slice(value_pad, corner, span_shape).reshape(head_count, -1, head_depth)
        live_mask = lax.dynamic_slice(inside, corner, mask_shape).reshape(1, 1, -1) > 0.5
        scores = jnp.where(live_mask, batched("hqd,hkd->hqk", q_rows, k_span) * score_scale, -jnp.inf)
        row_max = jnp.max(scores, axis=-1, keepdims=True)
        log_total = row_max + jnp.log(jnp.sum(jnp.exp(scores - row_max), axis=-1, keepdims=True))
        weights = jnp.exp(scores - log_total)
        weight_bf = rounded(weights)
        attended = batched("hqk,hkd->hqd", weight_bf, v_span)
        row_delta = jnp.sum(g_rows.astype(jnp.float32) * attended, axis=-1, keepdims=True)
        d_weights = batched("hqd,hkd->hqk", g_rows, v_span)
        d_scores = rounded(weights * (d_weights - row_delta))
        grad_rows = batched("hqk,hkd->hqd", d_scores, k_span) * score_scale
        return (grad_rows.astype(jnp.bfloat16).reshape(tile_shape), log_total.reshape(stat_tile), row_delta.reshape(stat_tile))

    tile_ids = jnp.arange(grid_f * grid_r * grid_c, dtype=jnp.int32)
    grad_tiles, total_tiles, delta_tiles = lax.map(query_tile, tile_ids)
    query_grad = tiles_back(grad_tiles, grid_f, grid_r, grid_c)
    log_totals = tiles_back(total_tiles, grid_f, grid_r, grid_c)
    deltas = tiles_back(delta_tiles, grid_f, grid_r, grid_c)
    query_pad = jnp.pad(query_in, border)
    grad_pad = jnp.pad(out_grad, border)
    total_pad = jnp.pad(log_totals, border[:4])
    delta_pad = jnp.pad(deltas, border[:4])

    def key_tile(tile_index):
        first, second, third = tile_place(tile_index)
        corner = corner_at(first, second, third, 5)
        corner_stat = corner_at(first, second, third, 4)
        k_rows = lax.dynamic_slice(key_in, corner, tile_shape).reshape(head_count, -1, head_depth)
        v_rows = lax.dynamic_slice(value_in, corner, tile_shape).reshape(head_count, -1, head_depth)
        q_span = lax.dynamic_slice(query_pad, corner, span_shape).reshape(head_count, -1, head_depth)
        g_span = lax.dynamic_slice(grad_pad, corner, span_shape).reshape(head_count, -1, head_depth)
        total_span = lax.dynamic_slice(total_pad, corner_stat, stat_span).reshape(head_count, -1, 1)
        delta_span = lax.dynamic_slice(delta_pad, corner_stat, stat_span).reshape(head_count, -1, 1)
        live_mask = lax.dynamic_slice(inside, corner, mask_shape).reshape(1, -1, 1) > 0.5
        scores = jnp.where(live_mask, batched("hqd,hkd->hqk", q_span, k_rows) * score_scale, -jnp.inf)
        weights = jnp.exp(scores - total_span)
        weight_bf = rounded(weights)
        d_weights = batched("hqd,hkd->hqk", g_span, v_rows)
        d_scores = rounded(weights * (d_weights - delta_span))
        key_part = batched("hqk,hqd->hkd", d_scores, q_span) * score_scale
        value_part = batched("hqk,hqd->hkd", weight_bf, g_span)
        return (key_part.astype(jnp.bfloat16).reshape(tile_shape), value_part.astype(jnp.bfloat16).reshape(tile_shape))

    key_tiles, value_tiles = lax.map(key_tile, tile_ids)
    key_grad = tiles_back(key_tiles, grid_f, grid_r, grid_c)
    value_grad = tiles_back(value_tiles, grid_f, grid_r, grid_c)
    return query_grad, key_grad, value_grad
```

```python
import functools
import math

import jax
import jax.numpy as jnp
from jax import lax
from jax.experimental import pallas as pl
from jax.experimental.pallas import tpu as pltpu
from jax.sharding import PartitionSpec as P

EDGES = ((0, 1), (0, -1), (1, 0), (-1, 0))
CORNERS = ((1, 1), (-1, -1), (1, -1), (-1, 1))
AROUND = EDGES + CORNERS
KEY_CHUNK = 256


def contract(a, b, dim_a, dim_b):
    return lax.dot_general(
        a, b, (((dim_a,), (dim_b,)), ((), ())), preferred_element_type=jnp.float32
    )


def stats_kernel(count, first, factor, live, *refs):
    q_ref, g_ref = refs[:2]
    kv_refs = refs[2 : 2 + count]
    out_ref = refs[-1]
    if first:
        shape = out_ref.shape[2:]
        out_ref[0, 0] = jnp.full(shape, -jnp.inf, jnp.float32)
        out_ref[0, 1] = jnp.zeros(shape, jnp.float32)
        out_ref[0, 2] = jnp.zeros(shape, jnp.float32)
    else:
        out_ref[...] = refs[2 + count][...]

    for slot, kv_ref in enumerate(kv_refs):

        def one(kv_ref=kv_ref):
            q = q_ref[0]
            g = g_ref[0]
            top, total, dot = out_ref[0, 0], out_ref[0, 1], out_ref[0, 2]
            keys = kv_ref.shape[2]
            for start in range(0, keys, KEY_CHUNK):
                k = kv_ref[0, 0, start : start + KEY_CHUNK]
                v = kv_ref[1, 0, start : start + KEY_CHUNK]
                s = contract(k, q, 1, 1)
                dp = contract(v, g, 1, 1)
                new = jnp.maximum(top, jnp.max(s, axis=0, keepdims=True))
                keep = jnp.exp2((top - new) * factor)
                e = jnp.exp2((s - new) * factor)
                total = total * keep + jnp.sum(e, axis=0, keepdims=True)
                dot = dot * keep + jnp.sum(e * dp, axis=0, keepdims=True)
                top = new
            out_ref[0, 0] = top
            out_ref[0, 1] = total
            out_ref[0, 2] = dot

        if first:
            one()
        else:
            pl.when(live[slot] > 0)(one)


def grads_kernel(count, own, first, factor, scale, live, *refs):
    q_ref, g_ref, st_ref = refs[:3]
    kv_refs = refs[3 : 3 + count]
    rest = refs[3 + count :]
    if first:
        acc_in, outs = None, rest
    else:
        acc_in, outs = rest[0], rest[1:]
    acc_ref = outs[-1]
    if first:
        acc_ref[...] = jnp.zeros_like(acc_ref)
    else:
        acc_ref[...] = acc_in[...]

    for slot, kv_ref in enumerate(kv_refs):

        def one(kv_ref=kv_ref, out_ref=outs[slot]):
            q = q_ref[0]
            g = g_ref[0]
            top, total, dot = st_ref[0, 0], st_ref[0, 1], st_ref[0, 2]
            log_total = top * factor + jnp.log2(total)
            delta = dot / total
            keys = kv_ref.shape[2]
            acc = acc_ref[0]
            for start in range(0, keys, KEY_CHUNK):
                rows = slice(start, start + KEY_CHUNK)
                k = kv_ref[0, 0, rows]
                v = kv_ref[1, 0, rows]
                s = contract(k, q, 1, 1)
                dp = contract(v, g, 1, 1)
                p = jnp.exp2(s * factor - log_total)
                ds = (p * (dp - delta)).astype(jnp.bfloat16)
                dv = contract(p.astype(jnp.bfloat16), g, 1, 0)
                dk = contract(ds, q, 1, 0) * scale
                acc = acc + contract(k, ds, 0, 0)
                out_ref[0, 0, rows] = dk.astype(out_ref.dtype)
                out_ref[1, 0, rows] = dv.astype(out_ref.dtype)
            acc_ref[0] = acc

        if own:
            one()
        else:
            pl.when(live[slot] > 0)(one)

    if own:
        dq_ref = outs[count]
        dq_ref[0] = (acc_ref[0] * scale).T.astype(dq_ref.dtype)


def per_head(shape, head_dim=0):
    block = tuple(1 if i == head_dim else n for i, n in enumerate(shape))
    return pl.BlockSpec(
        block, lambda h, *_: tuple(h if i == head_dim else 0 for i in range(len(shape)))
    )


def run_stats(live, q, g, blocks, stats, factor):
    heads, rows, depth = q.shape
    first = stats is None
    count = len(blocks)
    stat_shape = (heads, 3, 1, rows)
    args = [q, g, *blocks] + ([] if first else [stats])
    keys = blocks[0].shape[2]
    return pl.pallas_call(
        functools.partial(stats_kernel, count, first, factor),
        out_shape=jax.ShapeDtypeStruct(stat_shape, jnp.float32),
        grid_spec=pltpu.PrefetchScalarGridSpec(
            num_scalar_prefetch=1,
            grid=(heads,),
            in_specs=[per_head(a.shape) for a in (q, g)]
            + [per_head(b.shape, 1) for b in blocks]
            + ([] if first else [per_head(stat_shape)]),
            out_specs=per_head(stat_shape),
        ),
        cost_estimate=pl.CostEstimate(
            flops=4 * count * heads * rows * keys * depth,
            bytes_accessed=(2 + 2 * count) * heads * rows * depth * 2,
            transcendentals=count * heads * rows * keys,
        ),
        name="stats",
    )(live, *args)


def run_grads(live, q, g, stats, blocks, acc, factor, scale, own=False):
    heads, rows, depth = q.shape
    first = acc is None
    count = len(blocks)
    acc_shape = (heads, depth, rows)
    args = [q, g, stats, *blocks] + ([] if first else [acc])
    part = jnp.float32 if own else jnp.bfloat16
    keys = blocks[0].shape[2]
    out_shape = [jax.ShapeDtypeStruct(b.shape, part) for b in blocks]
    out_specs = [per_head(b.shape, 1) for b in blocks]
    if own:
        out_shape.append(jax.ShapeDtypeStruct(q.shape, jnp.bfloat16))
        out_specs.append(per_head(q.shape))
    out_shape.append(jax.ShapeDtypeStruct(acc_shape, jnp.float32))
    out_specs.append(per_head(acc_shape))
    return pl.pallas_call(
        functools.partial(grads_kernel, count, own, first, factor, scale),
        out_shape=out_shape,
        grid_spec=pltpu.PrefetchScalarGridSpec(
            num_scalar_prefetch=1,
            grid=(heads,),
            in_specs=[per_head(a.shape) for a in (q, g, stats)]
            + [per_head(b.shape, 1) for b in blocks]
            + ([] if first else [per_head(acc_shape)]),
            out_specs=out_specs,
        ),
        cost_estimate=pl.CostEstimate(
            flops=10 * count * heads * rows * keys * depth,
            bytes_accessed=(2 + 4 * count) * heads * rows * depth * 2,
            transcendentals=count * heads * rows * keys,
        ),
        name="grads",
    )(live, *args)


def moved(x, step, sizes):
    frames, rows = sizes
    route = []
    for f in range(frames):
        for r in range(rows):
            to_f, to_r = f + step[0], r + step[1]
            if 0 <= to_f < frames and 0 <= to_r < rows:
                route.append((f * rows + r, to_f * rows + to_r))
    return lax.ppermute(x, ("tm", "height"), route)


def local(query_in, key_in, value_in, out_grad):
    shape = query_in.shape
    heads, depth = shape[0], shape[-1]
    flat = (heads, math.prod(shape[1:4]), depth)
    scale = depth**-0.5
    factor = scale * math.log2(math.e)
    q, g = query_in.reshape(flat), out_grad.reshape(flat)
    kv = jnp.stack([key_in.reshape(flat), value_in.reshape(flat)])
    sizes = (lax.axis_size("tm"), lax.axis_size("height"))
    at = (lax.axis_index("tm"), lax.axis_index("height"))

    def lives(steps):
        flags = [
            (at[0] + f >= 0) & (at[0] + f < sizes[0]) & (at[1] + r >= 0) & (at[1] + r < sizes[1])
            for f, r in steps
        ]
        return jnp.stack(flags).astype(jnp.int32)

    near = {step: moved(kv, (-step[0], -step[1]), sizes) for step in AROUND}
    one = jnp.ones((1,), jnp.int32)
    stats = run_stats(one, q, g, [kv], None, factor)
    stats = run_stats(lives(EDGES), q, g, [near[s] for s in EDGES], stats, factor)
    stats = run_stats(lives(CORNERS), q, g, [near[s] for s in CORNERS], stats, factor)

    acc = None
    back = []
    for steps in (CORNERS[:2], CORNERS[2:], EDGES[:2], EDGES[2:]):
        *parts, acc = run_grads(
            lives(steps), q, g, stats, [near[s] for s in steps], acc, factor, scale
        )
        back += [moved(part, step, sizes) for part, step in zip(parts, steps)]
    total, dq, _ = run_grads(one, q, g, stats, [kv], acc, factor, scale, own=True)
    for part in back:
        total = total + part.astype(jnp.float32)
    total = total.astype(jnp.bfloat16)
    return dq.reshape(shape), total[0].reshape(shape), total[1].reshape(shape)


def solution(mesh):
    spec = P("head", "tm", "height", None, None)
    return jax.shard_map(
        local, mesh=mesh, in_specs=(spec,) * 4, out_specs=(spec,) * 3, check_vma=False
    )
```

```python
import functools
import math

import jax
import jax.numpy as jnp
from jax import lax
from jax.experimental import pallas as pl
from jax.experimental.pallas import tpu as pltpu
from jax.sharding import PartitionSpec as P

KEY_CHUNK_STATS = 128
KEY_CHUNK_GRADS = 512
VMEM = pl.BlockSpec(memory_space=pltpu.VMEM)
SMEM = pl.BlockSpec(memory_space=pltpu.SMEM)


def contract(a, b, dim_a, dim_b):
    return lax.dot_general(
        a, b, (((dim_a,), (dim_b,)), ((), ())), preferred_element_type=jnp.float32
    )


def guarded(live, flag, body):
    if flag is None:
        body()
    else:
        pl.when(live[flag] > 0)(body)


def stats_kernel(flags, first, factor, live, q_ref, g_ref, *refs):
    kv_refs, out_ref = refs[: len(flags)], refs[-1]
    heads = q_ref.shape[0]
    if first:
        for h in range(heads):
            shape = out_ref.shape[2:]
            out_ref[h, 0] = jnp.full(shape, -jnp.inf, jnp.float32)
            out_ref[h, 1] = jnp.zeros(shape, jnp.float32)
            out_ref[h, 2] = jnp.zeros(shape, jnp.float32)
    else:
        out_ref[...] = refs[len(flags)][...]

    def one(kv_ref, block):
        keys = kv_ref.shape[3]
        for h in range(heads):
            q, g = q_ref[h], g_ref[h]
            top, total, dot = out_ref[h, 0], out_ref[h, 1], out_ref[h, 2]
            for start in range(0, keys, KEY_CHUNK_STATS):
                rows = slice(start, start + KEY_CHUNK_STATS)
                s = contract(kv_ref[block, 0, h, rows], q, 1, 1)
                dp = contract(kv_ref[block, 1, h, rows], g, 1, 1)
                new = jnp.maximum(top, jnp.max(s, axis=0, keepdims=True))
                keep = jnp.exp2((top - new) * factor)
                e = jnp.exp2((s - new) * factor)
                total = total * keep + jnp.sum(e, axis=0, keepdims=True)
                dot = dot * keep + jnp.sum(e * dp, axis=0, keepdims=True)
                top = new
            out_ref[h, 0], out_ref[h, 1], out_ref[h, 2] = top, total, dot

    for kv_ref, kv_flags in zip(kv_refs, flags):
        for block, flag in enumerate(kv_flags):
            guarded(live, flag, functools.partial(one, kv_ref, block))


def grads_kernel(flags, first, last, factor, scale, live, q_ref, g_ref, st_ref, *refs):
    count = len(flags)
    kv_refs, refs = refs[:count], refs[count:]
    acc_in, refs = (None, refs) if first else (refs[0], refs[1:])
    out_refs, acc_ref = refs[:count], refs[count]
    heads = q_ref.shape[0]
    if first:
        acc_ref[...] = jnp.zeros_like(acc_ref)
    else:
        acc_ref[...] = acc_in[...]

    def one(kv_ref, out_ref, block):
        keys = kv_ref.shape[3]
        for h in range(heads):
            q, g = q_ref[h], g_ref[h]
            log_total = st_ref[h, 0] * factor + jnp.log2(st_ref[h, 1])
            delta = st_ref[h, 2] / st_ref[h, 1]
            for start in range(0, keys, KEY_CHUNK_GRADS):
                rows = slice(start, start + KEY_CHUNK_GRADS)
                k = kv_ref[block, 0, h, rows]
                s = contract(k, q, 1, 1)
                dp = contract(kv_ref[block, 1, h, rows], g, 1, 1)
                p = jnp.exp2(s * factor - log_total)
                ds = (p * (dp - delta)).astype(jnp.bfloat16)
                dv = contract(p.astype(jnp.bfloat16), g, 1, 0)
                dk = contract(ds, q, 1, 0) * scale
                acc_ref[h] += contract(k, ds, 0, 0)
                out_ref[block, 0, h, rows] = dk.astype(out_ref.dtype)
                out_ref[block, 1, h, rows] = dv.astype(out_ref.dtype)

    def none(out_ref, block):
        out_ref[block] = jnp.zeros(out_ref.shape[1:], out_ref.dtype)

    for kv_ref, out_ref, kv_flags in zip(kv_refs, out_refs, flags):
        for block, flag in enumerate(kv_flags):
            guarded(live, flag, functools.partial(one, kv_ref, out_ref, block))
            if flag is not None:
                pl.when(live[flag] == 0)(functools.partial(none, out_ref, block))

    if last:
        dq_ref = refs[count + 1]
        for h in range(heads):
            dq_ref[h] = (acc_ref[h] * scale).T.astype(dq_ref.dtype)


def run_stats(live, q, g, blocks, flags, stats, factor, cost=1000):
    heads, rows, _ = q.shape
    first = stats is None
    args = [live, q, g, *blocks] + ([] if first else [stats])
    return pl.pallas_call(
        functools.partial(stats_kernel, flags, first, factor),
        out_shape=jax.ShapeDtypeStruct((heads, 3, 1, rows), jnp.float32),
        in_specs=[SMEM] + [VMEM] * (len(args) - 1),
        out_specs=VMEM,
        cost_estimate=pl.CostEstimate(flops=cost, bytes_accessed=1000, transcendentals=0),
        name="stats",
    )(*args)


def run_grads(live, q, g, stats, blocks, flags, acc, factor, scale, part, last=False):
    heads, rows, depth = q.shape
    first = acc is None
    args = [live, q, g, stats, *blocks] + ([] if first else [acc])
    out_shape = [jax.ShapeDtypeStruct(b.shape, part) for b in blocks]
    out_shape.append(jax.ShapeDtypeStruct((heads, depth, rows), jnp.float32))
    aliases = {} if first else {len(args) - 1: len(blocks)}
    if last:
        out_shape.append(jax.ShapeDtypeStruct(q.shape, jnp.bfloat16))
    return pl.pallas_call(
        functools.partial(grads_kernel, flags, first, last, factor, scale),
        out_shape=out_shape,
        in_specs=[SMEM] + [VMEM] * (len(args) - 1),
        out_specs=[VMEM] * len(out_shape),
        input_output_aliases=aliases,
        cost_estimate=pl.CostEstimate(flops=1000, bytes_accessed=1000, transcendentals=0),
        name="grads",
    )(*args)


def relay_kernel(own_a, own_b, from_up, from_down, out_a, out_b):
    for block, (own, out) in enumerate(((own_a, out_a), (own_b, out_b))):
        out[0] = (
            own[0]
            + from_up[block].astype(jnp.float32)
            + from_down[block].astype(jnp.float32)
        ).astype(out.dtype)


def run_relay(own_a, own_b, from_up, from_down):
    return pl.pallas_call(
        relay_kernel,
        out_shape=[jax.ShapeDtypeStruct(own_a.shape, jnp.bfloat16)] * 2,
        in_specs=[VMEM] * 4,
        out_specs=[VMEM] * 2,
        cost_estimate=pl.CostEstimate(flops=1000, bytes_accessed=1000, transcendentals=0),
        name="relay",
    )(own_a, own_b, from_up, from_down)


def total_kernel(own, *refs):
    parts, outs = refs[:-2], refs[-2:]
    for which, out in enumerate(outs):
        total = own[0, which]
        for part in parts:
            total = total + part[0, which].astype(jnp.float32)
        out[...] = total.astype(out.dtype)


def run_total(own, parts):
    return pl.pallas_call(
        total_kernel,
        out_shape=[jax.ShapeDtypeStruct(own.shape[2:], jnp.bfloat16)] * 2,
        in_specs=[VMEM] * (1 + len(parts)),
        out_specs=[VMEM] * 2,
        cost_estimate=pl.CostEstimate(flops=1000, bytes_accessed=1000, transcendentals=0),
        name="total",
    )(own, *parts)


def moved(x, stage, step, sizes):
    frames, rows, heads = sizes
    route = []
    for f in range(frames):
        for r in range(rows):
            for h in range(heads):
                along_rows = (h + stage) % 2
                to_f, to_r = f + step * (1 - along_rows), r + step * along_rows
                if 0 <= to_f < frames and 0 <= to_r < rows:
                    route.append(
                        ((f * rows + r) * heads + h, (to_f * rows + to_r) * heads + h)
                    )
    return lax.ppermute(x, ("tm", "height", "head"), route)


def local(query_in, key_in, value_in, out_grad):
    shape = query_in.shape
    heads, depth = shape[0], shape[-1]
    flat = (heads, math.prod(shape[1:4]), depth)
    scale = depth**-0.5
    factor = scale * math.log2(math.e)
    q, g = query_in.reshape(flat), out_grad.reshape(flat)
    kv = jnp.stack([key_in.reshape(flat), value_in.reshape(flat)])[None]
    sizes = tuple(lax.axis_size(a) for a in ("tm", "height", "head"))
    frame, row = lax.axis_index("tm"), lax.axis_index("height")
    frames_first = lax.axis_index("head") % 2 == 0
    place = (jnp.where(frames_first, frame, row), jnp.where(frames_first, row, frame))
    size = (
        jnp.where(frames_first, sizes[0], sizes[1]),
        jnp.where(frames_first, sizes[1], sizes[0]),
    )
    up = [(place[i] + 1 < size[i]).astype(jnp.int32) for i in (0, 1)]
    down = [(place[i] > 0).astype(jnp.int32) for i in (0, 1)]
    live = jnp.stack(
        [
            up[0], down[0], up[1], down[1],
            up[1] * up[0], up[1] * down[0], down[1] * up[0], down[1] * down[0],
        ]
    )

    first_up, first_down = moved(kv, 0, -1, sizes), moved(kv, 0, 1, sizes)
    second_up, second_down = moved(kv, 1, -1, sizes), moved(kv, 1, 1, sizes)
    stats = run_stats(live, q, g, [kv], [[None]], None, factor)
    first_up, first_down, stats = lax.optimization_barrier((first_up, first_down, stats))
    both = jnp.concatenate([first_up, first_down])
    corner_up, corner_down = moved(both, 1, -1, sizes), moved(both, 1, 1, sizes)

    near, near_flags = [first_up, first_down, kv], [[0], [1], [None]]
    side, side_flags = [second_up, second_down], [[2], [3]]
    corner, corner_flags = [corner_up, corner_down], [[4, 5], [6, 7]]
    stats = run_stats(live, q, g, near[:2], near_flags[:2], stats, factor)
    stats = run_stats(live, q, g, side, side_flags, stats, factor, cost=20 * 10**12)
    stats = run_stats(live, q, g, [corner_up], [[4, 5]], stats, factor)
    stats = run_stats(live, q, g, [corner_down], [[6, 7]], stats, factor)

    grads = functools.partial(run_grads, live, q, g, stats)
    low = jnp.bfloat16
    part_up, part_down, acc = grads(corner, corner_flags, None, factor, scale, low)
    back_down = moved(part_up, 1, 1, sizes)
    back_up = moved(part_down, 1, -1, sizes)
    side_up, side_down, acc = grads(side, side_flags, acc, factor, scale, low)
    total_parts = [moved(side_up, 1, 1, sizes), moved(side_down, 1, -1, sizes)]
    own_up, own_down, own, _, dq = grads(
        near, near_flags, acc, factor, scale, jnp.float32, last=True
    )
    send_up, send_down = run_relay(own_up, own_down, back_up, back_down)
    total_parts += [moved(send_up, 0, 1, sizes), moved(send_down, 0, -1, sizes)]
    dk, dv = run_total(own, total_parts)
    return dq.reshape(shape), dk.reshape(shape), dv.reshape(shape)


def solution(mesh):
    spec = P("head", "tm", "height", None, None)
    return jax.shard_map(
        local, mesh=mesh, in_specs=(spec,) * 4, out_specs=(spec,) * 3, check_vma=False
    )
```

```python
import functools
import math

import jax
import jax.numpy as jnp
from jax import lax
from jax.experimental import pallas as pl
from jax.experimental.pallas import tpu as pltpu
from jax.sharding import PartitionSpec as P

KEY_CHUNK_STATS = 128
KEY_CHUNK_GRADS = 512
VMEM_LIMIT = 16 << 20
VMEM = pl.BlockSpec(memory_space=pltpu.VMEM)
SMEM = pl.BlockSpec(memory_space=pltpu.SMEM)


def contract(a, b, dim_a, dim_b):
    return lax.dot_general(
        a, b, (((dim_a,), (dim_b,)), ((), ())), preferred_element_type=jnp.float32
    )


def shown(live, flag, value, other):
    return value if flag is None else jnp.where(live[flag] > 0, value, other)


def stats_kernel(flags, first, factor, live, q_ref, g_ref, *refs):
    kv_refs, out_ref = refs[: len(flags)], refs[-1]
    for h in range(q_ref.shape[0]):
        q, g = q_ref[h], g_ref[h]
        if first:
            top = jnp.full(out_ref.shape[2:], -jnp.inf, jnp.float32)
            total = jnp.zeros_like(top)
            dot = jnp.zeros_like(top)
        else:
            top, total, dot = (refs[len(flags)][h, i] for i in range(3))
        for kv_ref, kv_flags in zip(kv_refs, flags):
            for block, flag in enumerate(kv_flags):
                for start in range(0, kv_ref.shape[3], KEY_CHUNK_STATS):
                    rows = slice(start, start + KEY_CHUNK_STATS)
                    s = contract(kv_ref[block, 0, h, rows], q, 1, 1)
                    dp = contract(kv_ref[block, 1, h, rows], g, 1, 1)
                    high = shown(live, flag, jnp.max(s, axis=0, keepdims=True), -jnp.inf)
                    new = jnp.maximum(top, high)
                    keep = jnp.exp2((top - new) * factor)
                    e = jnp.exp2((s - new) * factor)
                    more = jnp.sum(e, axis=0, keepdims=True)
                    total = total * keep + shown(live, flag, more, 0.0)
                    more = jnp.sum(e * dp, axis=0, keepdims=True)
                    dot = dot * keep + shown(live, flag, more, 0.0)
                    top = new
        out_ref[h, 0], out_ref[h, 1], out_ref[h, 2] = top, total, dot


def grads_kernel(flags, first, last, factor, scale, live, q_ref, g_ref, st_ref, *refs):
    count = len(flags)
    kv_refs, refs = refs[:count], refs[count:]
    acc_in, refs = (None, refs) if first else (refs[0], refs[1:])
    out_refs, end_ref = refs[:count], refs[count]
    for h in range(q_ref.shape[0]):
        q, g = q_ref[h], g_ref[h]
        log_total = st_ref[h, 0] * factor + jnp.log2(st_ref[h, 1])
        delta = st_ref[h, 2] / st_ref[h, 1]
        acc = jnp.zeros((q.shape[1], q.shape[0]), jnp.float32) if first else acc_in[h]
        for kv_ref, out_ref, kv_flags in zip(kv_refs, out_refs, flags):
            for block, flag in enumerate(kv_flags):
                low = shown(live, flag, log_total, jnp.inf)
                for start in range(0, kv_ref.shape[3], KEY_CHUNK_GRADS):
                    rows = slice(start, start + KEY_CHUNK_GRADS)
                    k = kv_ref[block, 0, h, rows]
                    s = contract(k, q, 1, 1)
                    dp = contract(kv_ref[block, 1, h, rows], g, 1, 1)
                    p = jnp.exp2(s * factor - low)
                    ds = (p * (dp - delta)).astype(jnp.bfloat16)
                    dv = contract(p.astype(jnp.bfloat16), g, 1, 0)
                    dk = contract(ds, q, 1, 0) * scale
                    acc = acc + contract(k, ds, 0, 0)
                    out_ref[block, 0, h, rows] = dk.astype(out_ref.dtype)
                    out_ref[block, 1, h, rows] = dv.astype(out_ref.dtype)
        if last:
            end_ref[h] = (acc * scale).T.astype(jnp.bfloat16)
        else:
            end_ref[h] = acc


def run_stats(live, q, g, blocks, flags, stats, factor, cost=1000):
    heads, rows, _ = q.shape
    first = stats is None
    args = [live, q, g, *blocks] + ([] if first else [stats])
    return pl.pallas_call(
        functools.partial(stats_kernel, flags, first, factor),
        out_shape=jax.ShapeDtypeStruct((heads, 3, 1, rows), jnp.float32),
        in_specs=[SMEM] + [VMEM] * (len(args) - 1),
        out_specs=VMEM,
        cost_estimate=pl.CostEstimate(flops=cost, bytes_accessed=1000, transcendentals=0),
        compiler_params=pltpu.CompilerParams(vmem_limit_bytes=VMEM_LIMIT),
        name="stats",
    )(*args)


def run_grads(live, q, g, stats, blocks, flags, acc, factor, scale, part, last=False):
    heads, rows, depth = q.shape
    first = acc is None
    args = [live, q, g, stats, *blocks] + ([] if first else [acc])
    out_shape = [jax.ShapeDtypeStruct(b.shape, part) for b in blocks]
    aliases = {}
    if last:
        out_shape.append(jax.ShapeDtypeStruct(q.shape, jnp.bfloat16))
    else:
        out_shape.append(jax.ShapeDtypeStruct((heads, depth, rows), jnp.float32))
        aliases = {} if first else {len(args) - 1: len(blocks)}
    return pl.pallas_call(
        functools.partial(grads_kernel, flags, first, last, factor, scale),
        out_shape=out_shape,
        in_specs=[SMEM] + [VMEM] * (len(args) - 1),
        out_specs=[VMEM] * len(out_shape),
        input_output_aliases=aliases,
        cost_estimate=pl.CostEstimate(flops=1000, bytes_accessed=1000, transcendentals=0),
        compiler_params=pltpu.CompilerParams(vmem_limit_bytes=VMEM_LIMIT),
        name="grads",
    )(*args)


def relay_kernel(own_a, own_b, from_up, from_down, out_a, out_b):
    for block, (own, out) in enumerate(((own_a, out_a), (own_b, out_b))):
        out[0] = (
            own[0]
            + from_up[block].astype(jnp.float32)
            + from_down[block].astype(jnp.float32)
        ).astype(out.dtype)


def run_relay(own_a, own_b, from_up, from_down):
    return pl.pallas_call(
        relay_kernel,
        out_shape=[jax.ShapeDtypeStruct(own_a.shape, jnp.bfloat16)] * 2,
        in_specs=[VMEM] * 4,
        out_specs=[VMEM] * 2,
        cost_estimate=pl.CostEstimate(flops=1000, bytes_accessed=1000, transcendentals=0),
        compiler_params=pltpu.CompilerParams(vmem_limit_bytes=VMEM_LIMIT),
        name="relay",
    )(own_a, own_b, from_up, from_down)


def total_kernel(own, *refs):
    parts, outs = refs[:-2], refs[-2:]
    for which, out in enumerate(outs):
        total = own[0, which]
        for part in parts:
            total = total + part[0, which].astype(jnp.float32)
        out[...] = total.astype(out.dtype)


def run_total(own, parts):
    return pl.pallas_call(
        total_kernel,
        out_shape=[jax.ShapeDtypeStruct(own.shape[2:], jnp.bfloat16)] * 2,
        in_specs=[VMEM] * (1 + len(parts)),
        out_specs=[VMEM] * 2,
        cost_estimate=pl.CostEstimate(flops=1000, bytes_accessed=1000, transcendentals=0),
        compiler_params=pltpu.CompilerParams(vmem_limit_bytes=VMEM_LIMIT),
        name="total",
    )(own, *parts)


def moved(x, stage, step, sizes):
    frames, rows, heads = sizes
    route = []
    for f in range(frames):
        for r in range(rows):
            for h in range(heads):
                along_rows = (h + stage) % 2
                to_f, to_r = f + step * (1 - along_rows), r + step * along_rows
                if 0 <= to_f < frames and 0 <= to_r < rows:
                    route.append(
                        ((f * rows + r) * heads + h, (to_f * rows + to_r) * heads + h)
                    )
    return lax.ppermute(x, ("tm", "height", "head"), route)


def local(query_in, key_in, value_in, out_grad):
    shape = query_in.shape
    heads, depth = shape[0], shape[-1]
    flat = (heads, math.prod(shape[1:4]), depth)
    scale = depth**-0.5
    factor = scale * math.log2(math.e)
    q, g = query_in.reshape(flat), out_grad.reshape(flat)
    kv = jnp.stack([key_in.reshape(flat), value_in.reshape(flat)])[None]
    sizes = tuple(lax.axis_size(a) for a in ("tm", "height", "head"))
    frame, row = lax.axis_index("tm"), lax.axis_index("height")
    frames_first = lax.axis_index("head") % 2 == 0
    place = (jnp.where(frames_first, frame, row), jnp.where(frames_first, row, frame))
    size = (
        jnp.where(frames_first, sizes[0], sizes[1]),
        jnp.where(frames_first, sizes[1], sizes[0]),
    )
    up = [(place[i] + 1 < size[i]).astype(jnp.int32) for i in (0, 1)]
    down = [(place[i] > 0).astype(jnp.int32) for i in (0, 1)]
    live = jnp.stack(
        [
            up[0], down[0], up[1], down[1],
            up[1] * up[0], up[1] * down[0], down[1] * up[0], down[1] * down[0],
        ]
    )

    first_up, first_down = moved(kv, 0, -1, sizes), moved(kv, 0, 1, sizes)
    second_up, second_down = moved(kv, 1, -1, sizes), moved(kv, 1, 1, sizes)
    stats = run_stats(live, q, g, [kv], [[None]], None, factor)
    first_up, first_down, stats = lax.optimization_barrier((first_up, first_down, stats))
    both = jnp.concatenate([first_up, first_down])
    corner_up, corner_down = moved(both, 1, -1, sizes), moved(both, 1, 1, sizes)

    near, near_flags = [first_up, first_down, kv], [[0], [1], [None]]
    side, side_flags = [second_up, second_down], [[2], [3]]
    corner, corner_flags = [corner_up, corner_down], [[4, 5], [6, 7]]
    stats = run_stats(live, q, g, near[:2], near_flags[:2], stats, factor)
    stats = run_stats(live, q, g, side, side_flags, stats, factor, cost=20 * 10**12)
    stats = run_stats(live, q, g, [corner_up], [[4, 5]], stats, factor)
    stats = run_stats(live, q, g, [corner_down], [[6, 7]], stats, factor)

    grads = functools.partial(run_grads, live, q, g, stats)
    low = jnp.bfloat16
    part_up, part_down, acc = grads(corner, corner_flags, None, factor, scale, low)
    back_down = moved(part_up, 1, 1, sizes)
    back_up = moved(part_down, 1, -1, sizes)
    side_up, side_down, acc = grads(side, side_flags, acc, factor, scale, low)
    total_parts = [moved(side_up, 1, 1, sizes), moved(side_down, 1, -1, sizes)]
    own_up, own_down, own, dq = grads(
        near, near_flags, acc, factor, scale, jnp.float32, last=True
    )
    send_up, send_down = run_relay(own_up, own_down, back_up, back_down)
    total_parts += [moved(send_up, 0, 1, sizes), moved(send_down, 0, -1, sizes)]
    dk, dv = run_total(own, total_parts)
    return dq.reshape(shape), dk.reshape(shape), dv.reshape(shape)


def solution(mesh):
    spec = P("head", "tm", "height", None, None)
    return jax.shard_map(
        local, mesh=mesh, in_specs=(spec,) * 4, out_specs=(spec,) * 3, check_vma=False
    )
```

```python
import functools
import math

import jax
import jax.numpy as jnp
from jax import lax
from jax.experimental import pallas as pl
from jax.experimental.pallas import tpu as pltpu
from jax.sharding import PartitionSpec as P

KEY_CHUNK_STATS = 128
KEY_CHUNK_GRADS = 512
VMEM_LIMIT = 16 << 20
VMEM = pl.BlockSpec(memory_space=pltpu.VMEM)
SMEM = pl.BlockSpec(memory_space=pltpu.SMEM)


def contract(a, b, dim_a, dim_b):
    return lax.dot_general(
        a, b, (((dim_a,), (dim_b,)), ((), ())), preferred_element_type=jnp.float32
    )


def shown(live, flag, value, other):
    return value if flag is None else jnp.where(live[flag] > 0, value, other)


def stats_kernel(flags, first, factor, live, q_ref, g_ref, *refs):
    kv_refs, out_ref = refs[: len(flags)], refs[-1]
    for h in range(q_ref.shape[0]):
        q, g = q_ref[h], g_ref[h]
        if first:
            top = jnp.full(out_ref.shape[2:], -jnp.inf, jnp.float32)
            total = jnp.zeros_like(top)
            dot = jnp.zeros_like(top)
        else:
            top, total, dot = (refs[len(flags)][h, i] for i in range(3))
        for kv_ref, kv_flags in zip(kv_refs, flags):
            for block, flag in enumerate(kv_flags):
                for start in range(0, kv_ref.shape[3], KEY_CHUNK_STATS):
                    rows = slice(start, start + KEY_CHUNK_STATS)
                    s = contract(kv_ref[block, 0, h, rows], q, 1, 1)
                    dp = contract(kv_ref[block, 1, h, rows], g, 1, 1)
                    high = shown(live, flag, jnp.max(s, axis=0, keepdims=True), -jnp.inf)
                    new = jnp.maximum(top, high)
                    keep = jnp.exp2((top - new) * factor)
                    e = jnp.exp2((s - new) * factor)
                    more = jnp.sum(e, axis=0, keepdims=True)
                    total = total * keep + shown(live, flag, more, 0.0)
                    more = jnp.sum(e * dp, axis=0, keepdims=True)
                    dot = dot * keep + shown(live, flag, more, 0.0)
                    top = new
        out_ref[h, 0], out_ref[h, 1], out_ref[h, 2] = top, total, dot


def grads_kernel(flags, first, last, factor, scale, live, q_ref, g_ref, st_ref, *refs):
    count = len(flags)
    kv_refs, refs = refs[:count], refs[count:]
    acc_in, refs = (None, refs) if first else (refs[0], refs[1:])
    out_refs, end_ref = refs[:count], refs[count]
    for h in range(q_ref.shape[0]):
        q, g = q_ref[h], g_ref[h]
        log_total = st_ref[h, 0] * factor + jnp.log2(st_ref[h, 1])
        delta = st_ref[h, 2] / st_ref[h, 1]
        acc = jnp.zeros((q.shape[1], q.shape[0]), jnp.float32) if first else acc_in[h]
        for kv_ref, out_ref, kv_flags in zip(kv_refs, out_refs, flags):
            for block, flag in enumerate(kv_flags):
                low = shown(live, flag, log_total, jnp.inf)
                for start in range(0, kv_ref.shape[3], KEY_CHUNK_GRADS):
                    rows = slice(start, start + KEY_CHUNK_GRADS)
                    k = kv_ref[block, 0, h, rows]
                    s = contract(k, q, 1, 1)
                    dp = contract(kv_ref[block, 1, h, rows], g, 1, 1)
                    p = jnp.exp2(s * factor - low)
                    ds = (p * (dp - delta)).astype(jnp.bfloat16)
                    dv = contract(p.astype(jnp.bfloat16), g, 1, 0)
                    dk = contract(ds, q, 1, 0) * scale
                    acc = acc + contract(k, ds, 0, 0)
                    out_ref[block, 0, h, rows] = dk.astype(out_ref.dtype)
                    out_ref[block, 1, h, rows] = dv.astype(out_ref.dtype)
        if last:
            end_ref[h] = (acc * scale).T.astype(jnp.bfloat16)
        else:
            end_ref[h] = acc


def corner_kernel(
    flags, factor, scale, live, q_ref, g_ref, st_ref, *refs
):
    count = len(flags)
    kv_refs, out_refs = refs[:count], refs[count : 2 * count]
    end_ref, acc_ref, s_ref, dp_ref = refs[2 * count :]
    todo = [
        (kv_ref, out_ref, block, flag)
        for kv_ref, out_ref, kv_flags in zip(kv_refs, out_refs, flags)
        for block, flag in enumerate(kv_flags)
    ]
    for h in range(q_ref.shape[0]):
        q, g = q_ref[h], g_ref[h]
        top, total, dot = (st_ref[h, i] for i in range(3))
        for slot, (kv_ref, _, block, flag) in enumerate(todo):
            for start in range(0, kv_ref.shape[3], KEY_CHUNK_STATS):
                rows = slice(start, start + KEY_CHUNK_STATS)
                s = contract(kv_ref[block, 0, h, rows], q, 1, 1)
                dp = contract(kv_ref[block, 1, h, rows], g, 1, 1)
                s_ref[slot, rows] = s
                dp_ref[slot, rows] = dp
                high = shown(live, flag, jnp.max(s, axis=0, keepdims=True), -jnp.inf)
                new = jnp.maximum(top, high)
                keep = jnp.exp2((top - new) * factor)
                e = jnp.exp2((s - new) * factor)
                more = jnp.sum(e, axis=0, keepdims=True)
                total = total * keep + shown(live, flag, more, 0.0)
                more = jnp.sum(e * dp, axis=0, keepdims=True)
                dot = dot * keep + shown(live, flag, more, 0.0)
                top = new
        end_ref[h, 0], end_ref[h, 1], end_ref[h, 2] = top, total, dot
        log_total = top * factor + jnp.log2(total)
        delta = dot / total
        acc = jnp.zeros((q.shape[1], q.shape[0]), jnp.float32)
        for slot, (kv_ref, out_ref, block, flag) in enumerate(todo):
            low = shown(live, flag, log_total, jnp.inf)
            p = jnp.exp2(s_ref[slot] * factor - low)
            ds = (p * (dp_ref[slot] - delta)).astype(jnp.bfloat16)
            dv = contract(p.astype(jnp.bfloat16), g, 1, 0)
            dk = contract(ds, q, 1, 0) * scale
            acc = acc + contract(kv_ref[block, 0, h], ds, 0, 0)
            out_ref[block, 0, h] = dk.astype(out_ref.dtype)
            out_ref[block, 1, h] = dv.astype(out_ref.dtype)
        acc_ref[h] = acc


def run_corner(live, q, g, stats, blocks, flags, factor, scale):
    heads, rows, depth = q.shape
    count = sum(len(f) for f in flags)
    keys = blocks[0].shape[3]
    out_shape = [jax.ShapeDtypeStruct(b.shape, jnp.bfloat16) for b in blocks]
    out_shape.append(jax.ShapeDtypeStruct(stats.shape, jnp.float32))
    out_shape.append(jax.ShapeDtypeStruct((heads, depth, rows), jnp.float32))
    return pl.pallas_call(
        functools.partial(corner_kernel, flags, factor, scale),
        out_shape=out_shape,
        in_specs=[SMEM] + [VMEM] * (3 + len(blocks)),
        out_specs=[VMEM] * len(out_shape),
        scratch_shapes=[pltpu.VMEM((count, keys, rows), jnp.float32)] * 2,
        cost_estimate=pl.CostEstimate(flops=1000, bytes_accessed=1000, transcendentals=0),
        compiler_params=pltpu.CompilerParams(vmem_limit_bytes=2 * VMEM_LIMIT),
        name="corner",
    )(live, q, g, stats, *blocks)


def run_stats(live, q, g, blocks, flags, stats, factor, cost=1000):
    heads, rows, _ = q.shape
    first = stats is None
    args = [live, q, g, *blocks] + ([] if first else [stats])
    return pl.pallas_call(
        functools.partial(stats_kernel, flags, first, factor),
        out_shape=jax.ShapeDtypeStruct((heads, 3, 1, rows), jnp.float32),
        in_specs=[SMEM] + [VMEM] * (len(args) - 1),
        out_specs=VMEM,
        cost_estimate=pl.CostEstimate(flops=cost, bytes_accessed=1000, transcendentals=0),
        compiler_params=pltpu.CompilerParams(vmem_limit_bytes=VMEM_LIMIT),
        name="stats",
    )(*args)


def run_grads(live, q, g, stats, blocks, flags, acc, factor, scale, part, last=False):
    heads, rows, depth = q.shape
    first = acc is None
    args = [live, q, g, stats, *blocks] + ([] if first else [acc])
    out_shape = [jax.ShapeDtypeStruct(b.shape, part) for b in blocks]
    aliases = {}
    if last:
        out_shape.append(jax.ShapeDtypeStruct(q.shape, jnp.bfloat16))
    else:
        out_shape.append(jax.ShapeDtypeStruct((heads, depth, rows), jnp.float32))
        aliases = {} if first else {len(args) - 1: len(blocks)}
    return pl.pallas_call(
        functools.partial(grads_kernel, flags, first, last, factor, scale),
        out_shape=out_shape,
        in_specs=[SMEM] + [VMEM] * (len(args) - 1),
        out_specs=[VMEM] * len(out_shape),
        input_output_aliases=aliases,
        cost_estimate=pl.CostEstimate(flops=1000, bytes_accessed=1000, transcendentals=0),
        compiler_params=pltpu.CompilerParams(vmem_limit_bytes=VMEM_LIMIT),
        name="grads",
    )(*args)


def join_kernel(a_ref, b_ref, out_ref):
    out_ref[0] = a_ref[0]
    out_ref[1] = b_ref[0]


def run_join(a, b):
    return pl.pallas_call(
        join_kernel,
        out_shape=jax.ShapeDtypeStruct((2,) + a.shape[1:], a.dtype),
        in_specs=[VMEM] * 2,
        out_specs=VMEM,
        cost_estimate=pl.CostEstimate(flops=1000, bytes_accessed=1000, transcendentals=0),
        compiler_params=pltpu.CompilerParams(vmem_limit_bytes=VMEM_LIMIT),
        name="join",
    )(a, b)


def relay_kernel(own_a, own_b, from_a, from_b, out_a, out_b):
    for block, (own, out) in enumerate(((own_a, out_a), (own_b, out_b))):
        out[0] = (
            own[0]
            + from_a[block].astype(jnp.float32)
            + from_b[block].astype(jnp.float32)
        ).astype(out.dtype)


def run_relay(own_a, own_b, from_a, from_b):
    return pl.pallas_call(
        relay_kernel,
        out_shape=[jax.ShapeDtypeStruct(own_a.shape, jnp.bfloat16)] * 2,
        in_specs=[VMEM] * 4,
        out_specs=[VMEM] * 2,
        cost_estimate=pl.CostEstimate(flops=1000, bytes_accessed=1000, transcendentals=0),
        compiler_params=pltpu.CompilerParams(vmem_limit_bytes=VMEM_LIMIT),
        name="relay",
    )(own_a, own_b, from_a, from_b)


def total_kernel(own, *refs):
    parts, outs = refs[:-2], refs[-2:]
    for which, out in enumerate(outs):
        total = own[0, which]
        for part in parts:
            total = total + part[0, which].astype(jnp.float32)
        out[...] = total.astype(out.dtype)


def run_total(own, parts):
    return pl.pallas_call(
        total_kernel,
        out_shape=[jax.ShapeDtypeStruct(own.shape[2:], jnp.bfloat16)] * 2,
        in_specs=[VMEM] * (1 + len(parts)),
        out_specs=[VMEM] * 2,
        cost_estimate=pl.CostEstimate(flops=1000, bytes_accessed=1000, transcendentals=0),
        compiler_params=pltpu.CompilerParams(vmem_limit_bytes=VMEM_LIMIT),
        name="total",
    )(own, *parts)


def partner(at, pair):
    odd = at % 2
    return at + (1 - 2 * odd) * (1 - 2 * pair)


def swapped(x, stage, pair, sizes):
    frames, rows, heads = sizes
    route = []
    for f in range(frames):
        for r in range(rows):
            for h in range(heads):
                along_rows = (h + stage) % 2
                to_f = f if along_rows else partner(f, pair)
                to_r = partner(r, pair) if along_rows else r
                if 0 <= to_f < frames and 0 <= to_r < rows:
                    route.append(
                        ((f * rows + r) * heads + h, (to_f * rows + to_r) * heads + h)
                    )
    return lax.ppermute(x, ("tm", "height", "head"), route)


def local(query_in, key_in, value_in, out_grad):
    shape = query_in.shape
    heads, depth = shape[0], shape[-1]
    flat = (heads, math.prod(shape[1:4]), depth)
    scale = depth**-0.5
    factor = scale * math.log2(math.e)
    q, g = query_in.reshape(flat), out_grad.reshape(flat)
    kv = jnp.stack([key_in.reshape(flat), value_in.reshape(flat)])[None]
    sizes = tuple(lax.axis_size(a) for a in ("tm", "height", "head"))
    frame, row = lax.axis_index("tm"), lax.axis_index("height")
    frames_first = lax.axis_index("head") % 2 == 0
    place = (jnp.where(frames_first, frame, row), jnp.where(frames_first, row, frame))
    size = (
        jnp.where(frames_first, sizes[0], sizes[1]),
        jnp.where(frames_first, sizes[1], sizes[0]),
    )
    met = [[partner(place[i], pair) for pair in (0, 1)] for i in (0, 1)]
    first, second = [
        [((m >= 0) & (m < size[i])).astype(jnp.int32) for m in met[i]] for i in (0, 1)
    ]
    live = jnp.stack(first + second + [b * a for b in second for a in first])

    first_a, first_b = (swapped(kv, 0, pair, sizes) for pair in (0, 1))
    stats = run_stats(live, q, g, [kv], [[None]], None, factor)
    later, stats = lax.optimization_barrier((kv, stats))
    second_a, second_b = (swapped(later, 1, pair, sizes) for pair in (0, 1))
    both = run_join(first_a, first_b)
    corner_a, corner_b = (swapped(both, 1, pair, sizes) for pair in (0, 1))

    near, near_flags = [first_a, first_b, kv], [[0], [1], [None]]
    side, side_flags = [second_a, second_b], [[2], [3]]
    corner, corner_flags = [corner_a, corner_b], [[4, 5], [6, 7]]
    stats = run_stats(live, q, g, near[:2], near_flags[:2], stats, factor)
    stats = run_stats(live, q, g, side, side_flags, stats, factor, cost=20 * 10**12)
    part_a, part_b, stats, acc = run_corner(
        live, q, g, stats, corner, corner_flags, factor, scale
    )
    back_a, back_b = swapped(part_a, 1, 0, sizes), swapped(part_b, 1, 1, sizes)
    grads = functools.partial(run_grads, live, q, g, stats)
    side_a, side_b, acc = grads(side, side_flags, acc, factor, scale, jnp.bfloat16)
    total_parts = [swapped(side_a, 1, 0, sizes), swapped(side_b, 1, 1, sizes)]
    own_a, own_b, own, dq = grads(near, near_flags, acc, factor, scale, jnp.float32, last=True)
    send_a, send_b = run_relay(own_a, own_b, back_a, back_b)
    total_parts += [swapped(send_a, 0, 0, sizes), swapped(send_b, 0, 1, sizes)]
    dk, dv = run_total(own, total_parts)
    return dq.reshape(shape), dk.reshape(shape), dv.reshape(shape)


def solution(mesh):
    spec = P("head", "tm", "height", None, None)
    return jax.shard_map(
        local, mesh=mesh, in_specs=(spec,) * 4, out_specs=(spec,) * 3, check_vma=False
    )
```

```python
import functools
import math

import jax
import jax.numpy as jnp
from jax import lax
from jax.experimental import pallas as pl
from jax.experimental.pallas import tpu as pltpu
from jax.sharding import PartitionSpec as P

KEY_CHUNK_STATS = 128
VMEM_LIMIT = 16 << 20
VMEM = pl.BlockSpec(memory_space=pltpu.VMEM)
SMEM = pl.BlockSpec(memory_space=pltpu.SMEM)


def contract(a, b, dim_a, dim_b):
    return lax.dot_general(
        a, b, (((dim_a,), (dim_b,)), ((), ())), preferred_element_type=jnp.float32
    )


def shown(live, flag, value, other):
    return value if flag is None else jnp.where(live[flag] > 0, value, other)


def by_eight(x):
    return x.reshape(x.shape[0] // 8, 8, x.shape[1])


def stats_of(kv_refs, flags, factor, live, h, q, g, carried):
    top, total, dot = carried
    for kv_ref, kv_flags in zip(kv_refs, flags):
        for block, flag in enumerate(kv_flags):
            for start in range(0, kv_ref.shape[3], KEY_CHUNK_STATS):
                rows = slice(start, start + KEY_CHUNK_STATS)
                s = by_eight(contract(kv_ref[block, 0, h, rows], q, 1, 1))
                dp = by_eight(contract(kv_ref[block, 1, h, rows], g, 1, 1))
                new = jnp.maximum(top, shown(live, flag, jnp.max(s, axis=0), -jnp.inf))
                keep = jnp.exp2((top - new) * factor)
                e = jnp.exp2((s - new[None]) * factor)
                total = total * keep + shown(live, flag, jnp.sum(e, axis=0), 0.0)
                dot = dot * keep + shown(live, flag, jnp.sum(e * dp, axis=0), 0.0)
                top = new
    return top, total, dot


def stats_kernel(flags, first, factor, live, q_ref, g_ref, *refs):
    kv_refs, out_ref = refs[: len(flags)], refs[-1]
    for h in range(q_ref.shape[0]):
        if first:
            zero = jnp.zeros(out_ref.shape[2:], jnp.float32)
            carried = (jnp.full_like(zero, -jnp.inf), zero, zero)
        else:
            carried = tuple(refs[len(flags)][h, i] for i in range(3))
        result = stats_of(kv_refs, flags, factor, live, h, q_ref[h], g_ref[h], carried)
        out_ref[h, 0], out_ref[h, 1], out_ref[h, 2] = result


def grads_of(kv_refs, out_refs, flags, factor, scale, live, h, q, g, log_total, delta, acc):
    for kv_ref, out_ref, kv_flags in zip(kv_refs, out_refs, flags):
        for block, flag in enumerate(kv_flags):
            low = shown(live, flag, log_total, jnp.inf)
            k = kv_ref[block, 0, h]
            s = contract(k, q, 1, 1)
            dp = contract(kv_ref[block, 1, h], g, 1, 1)
            p = jnp.exp2(by_eight(s) * factor - low[None])
            ds = (p * (by_eight(dp) - delta[None])).reshape(s.shape).astype(jnp.bfloat16)
            dv = contract(p.reshape(s.shape).astype(jnp.bfloat16), g, 1, 0)
            dk = contract(ds, q, 1, 0) * scale
            acc = acc + contract(k, ds, 0, 0)
            out_ref[block, 0, h] = dk.astype(out_ref.dtype)
            out_ref[block, 1, h] = dv.astype(out_ref.dtype)
    return acc


def corner_kernel(flags, factor, scale, live, q_ref, g_ref, st_ref, *refs):
    count = len(flags)
    kv_refs, out_refs = refs[:count], refs[count : 2 * count]
    end_ref, acc_ref = refs[2 * count :]
    for h in range(q_ref.shape[0]):
        q, g = q_ref[h], g_ref[h]
        carried = tuple(st_ref[h, i] for i in range(3))
        top, total, dot = stats_of(kv_refs, flags, factor, live, h, q, g, carried)
        peak = jnp.max(top, axis=0, keepdims=True)
        share = jnp.exp2((top - peak) * factor)
        total = jnp.sum(share * total, axis=0, keepdims=True)
        dot = jnp.sum(share * dot, axis=0, keepdims=True)
        end_ref[h, 0] = jnp.broadcast_to(peak * factor + jnp.log2(total), top.shape)
        end_ref[h, 1] = jnp.broadcast_to(dot / total, top.shape)
        acc = jnp.zeros((q.shape[1], q.shape[0]), jnp.float32)
        acc_ref[h] = grads_of(
            kv_refs, out_refs, flags, factor, scale, live, h, q, g,
            end_ref[h, 0], end_ref[h, 1], acc,
        )


def grads_kernel(flags, last, factor, scale, live, q_ref, g_ref, end_ref, *refs):
    count = len(flags)
    kv_refs, acc_in = refs[:count], refs[count]
    out_refs, acc_ref = refs[count + 1 : 2 * count + 1], refs[2 * count + 1]
    for h in range(q_ref.shape[0]):
        acc = grads_of(
            kv_refs, out_refs, flags, factor, scale, live, h, q_ref[h], g_ref[h],
            end_ref[h, 0], end_ref[h, 1], acc_in[h],
        )
        if last:
            acc_ref[h] = (acc * scale).T.astype(jnp.bfloat16)
        else:
            acc_ref[h] = acc


def run_corner(live, q, g, stats, blocks, flags, factor, scale):
    heads, rows, depth = q.shape
    out_shape = [jax.ShapeDtypeStruct(b.shape, jnp.bfloat16) for b in blocks]
    out_shape.append(jax.ShapeDtypeStruct((heads, 2, 8, rows), jnp.float32))
    out_shape.append(jax.ShapeDtypeStruct((heads, depth, rows), jnp.float32))
    return pl.pallas_call(
        functools.partial(corner_kernel, flags, factor, scale),
        out_shape=out_shape,
        in_specs=[SMEM] + [VMEM] * (3 + len(blocks)),
        out_specs=[VMEM] * len(out_shape),
        cost_estimate=pl.CostEstimate(flops=1000, bytes_accessed=1000, transcendentals=0),
        compiler_params=pltpu.CompilerParams(vmem_limit_bytes=VMEM_LIMIT),
        name="corner",
    )(live, q, g, stats, *blocks)


def run_stats(live, q, g, blocks, flags, stats, factor, cost=1000):
    heads, rows, _ = q.shape
    first = stats is None
    args = [live, q, g, *blocks] + ([] if first else [stats])
    return pl.pallas_call(
        functools.partial(stats_kernel, flags, first, factor),
        out_shape=jax.ShapeDtypeStruct((heads, 3, 8, rows), jnp.float32),
        in_specs=[SMEM] + [VMEM] * (len(args) - 1),
        out_specs=VMEM,
        cost_estimate=pl.CostEstimate(flops=cost, bytes_accessed=1000, transcendentals=0),
        compiler_params=pltpu.CompilerParams(vmem_limit_bytes=VMEM_LIMIT),
        name="stats",
    )(*args)


def run_grads(live, q, g, ends, blocks, flags, acc, factor, scale, part, last=False):
    args = [live, q, g, ends, *blocks, acc]
    end = jax.ShapeDtypeStruct(*((q.shape, q.dtype) if last else (acc.shape, acc.dtype)))
    return pl.pallas_call(
        functools.partial(grads_kernel, flags, last, factor, scale),
        out_shape=[jax.ShapeDtypeStruct(b.shape, part) for b in blocks] + [end],
        in_specs=[SMEM] + [VMEM] * (len(args) - 1),
        out_specs=[VMEM] * (len(blocks) + 1),
        input_output_aliases={} if last else {len(args) - 1: len(blocks)},
        cost_estimate=pl.CostEstimate(flops=1000, bytes_accessed=1000, transcendentals=0),
        compiler_params=pltpu.CompilerParams(vmem_limit_bytes=VMEM_LIMIT),
        name="grads",
    )(*args)


def join_kernel(a_ref, b_ref, out_ref):
    out_ref[0] = a_ref[0]
    out_ref[1] = b_ref[0]


def run_join(a, b):
    return pl.pallas_call(
        join_kernel,
        out_shape=jax.ShapeDtypeStruct((2,) + a.shape[1:], a.dtype),
        in_specs=[VMEM] * 2,
        out_specs=VMEM,
        cost_estimate=pl.CostEstimate(flops=1000, bytes_accessed=1000, transcendentals=0),
        compiler_params=pltpu.CompilerParams(vmem_limit_bytes=VMEM_LIMIT),
        name="join",
    )(a, b)


def relay_kernel(own_a, own_b, from_a, from_b, out_a, out_b):
    for block, (own, out) in enumerate(((own_a, out_a), (own_b, out_b))):
        out[0] = (
            own[0]
            + from_a[block].astype(jnp.float32)
            + from_b[block].astype(jnp.float32)
        ).astype(out.dtype)


def run_relay(own_a, own_b, from_a, from_b):
    return pl.pallas_call(
        relay_kernel,
        out_shape=[jax.ShapeDtypeStruct(own_a.shape, jnp.bfloat16)] * 2,
        in_specs=[VMEM] * 4,
        out_specs=[VMEM] * 2,
        cost_estimate=pl.CostEstimate(flops=1000, bytes_accessed=1000, transcendentals=0),
        compiler_params=pltpu.CompilerParams(vmem_limit_bytes=VMEM_LIMIT),
        name="relay",
    )(own_a, own_b, from_a, from_b)


def total_kernel(own, *refs):
    parts, outs = refs[:-2], refs[-2:]
    for which, out in enumerate(outs):
        total = own[0, which]
        for part in parts:
            total = total + part[0, which].astype(jnp.float32)
        out[...] = total.astype(out.dtype)


def run_total(own, parts):
    return pl.pallas_call(
        total_kernel,
        out_shape=[jax.ShapeDtypeStruct(own.shape[2:], jnp.bfloat16)] * 2,
        in_specs=[VMEM] * (1 + len(parts)),
        out_specs=[VMEM] * 2,
        cost_estimate=pl.CostEstimate(flops=1000, bytes_accessed=1000, transcendentals=0),
        compiler_params=pltpu.CompilerParams(vmem_limit_bytes=VMEM_LIMIT),
        name="total",
    )(own, *parts)


def partner(at, pair):
    odd = at % 2
    return at + (1 - 2 * odd) * (1 - 2 * pair)


def swapped(x, stage, pair, sizes):
    frames, rows, heads = sizes
    route = []
    for f in range(frames):
        for r in range(rows):
            for h in range(heads):
                along_rows = (h + stage) % 2
                to_f = f if along_rows else partner(f, pair)
                to_r = partner(r, pair) if along_rows else r
                if 0 <= to_f < frames and 0 <= to_r < rows:
                    route.append(
                        ((f * rows + r) * heads + h, (to_f * rows + to_r) * heads + h)
                    )
    return lax.ppermute(x, ("tm", "height", "head"), route)


def local(query_in, key_in, value_in, out_grad):
    shape = query_in.shape
    heads, depth = shape[0], shape[-1]
    flat = (heads, math.prod(shape[1:4]), depth)
    scale = depth**-0.5
    factor = scale * math.log2(math.e)
    q, g = query_in.reshape(flat), out_grad.reshape(flat)
    kv = jnp.stack([key_in.reshape(flat), value_in.reshape(flat)])[None]
    sizes = tuple(lax.axis_size(a) for a in ("tm", "height", "head"))
    frame, row = lax.axis_index("tm"), lax.axis_index("height")
    frames_first = lax.axis_index("head") % 2 == 0
    place = (jnp.where(frames_first, frame, row), jnp.where(frames_first, row, frame))
    size = (
        jnp.where(frames_first, sizes[0], sizes[1]),
        jnp.where(frames_first, sizes[1], sizes[0]),
    )
    met = [[partner(place[i], pair) for pair in (0, 1)] for i in (0, 1)]
    first, second = [
        [((m >= 0) & (m < size[i])).astype(jnp.int32) for m in met[i]] for i in (0, 1)
    ]
    live = jnp.stack(first + second + [b * a for b in second for a in first])

    first_a, first_b = (swapped(kv, 0, pair, sizes) for pair in (0, 1))
    stats = run_stats(live, q, g, [kv], [[None]], None, factor)
    later, stats, first_a = lax.optimization_barrier((kv, stats, first_a))
    second_a, second_b = (swapped(later, 1, pair, sizes) for pair in (0, 1))
    both = run_join(first_a, first_b)
    corner_a, corner_b = (swapped(both, 1, pair, sizes) for pair in (0, 1))

    near, near_flags = [first_a, first_b, kv], [[0], [1], [None]]
    side, side_flags = [second_a, second_b], [[2], [3]]
    corner, corner_flags = [corner_a, corner_b], [[4, 5], [6, 7]]
    stats = run_stats(live, q, g, near[:2], near_flags[:2], stats, factor)
    stats = run_stats(live, q, g, side, side_flags, stats, factor, cost=20 * 10**12)
    part_a, part_b, ends, acc = run_corner(
        live, q, g, stats, corner, corner_flags, factor, scale
    )
    back_a, back_b = swapped(part_a, 1, 0, sizes), swapped(part_b, 1, 1, sizes)
    grads = functools.partial(run_grads, live, q, g, ends)
    side_a, side_b, acc = grads(side, side_flags, acc, factor, scale, jnp.bfloat16)
    total_parts = [swapped(side_a, 1, 0, sizes), swapped(side_b, 1, 1, sizes)]
    own_a, own_b, own, dq = grads(near, near_flags, acc, factor, scale, jnp.float32, last=True)
    send_a, send_b = run_relay(own_a, own_b, back_a, back_b)
    total_parts += [swapped(send_a, 0, 0, sizes), swapped(send_b, 0, 1, sizes)]
    dk, dv = run_total(own, total_parts)
    return dq.reshape(shape), dk.reshape(shape), dv.reshape(shape)


def solution(mesh):
    spec = P("head", "tm", "height", None, None)
    return jax.shard_map(
        local, mesh=mesh, in_specs=(spec,) * 4, out_specs=(spec,) * 3, check_vma=False
    )
```

```python
import functools
import math

import jax
import jax.numpy as jnp
from jax import lax
from jax.experimental import pallas as pl
from jax.experimental.pallas import tpu as pltpu
from jax.sharding import PartitionSpec as P

KEY_CHUNK_STATS = 128
VMEM_LIMIT = 16 << 20
VMEM = pl.BlockSpec(memory_space=pltpu.VMEM)
SMEM = pl.BlockSpec(memory_space=pltpu.SMEM)


def contract(a, b, dim_a, dim_b):
    return lax.dot_general(
        a, b, (((dim_a,), (dim_b,)), ((), ())), preferred_element_type=jnp.float32
    )


def shown(live, flag, value, other):
    return value if flag is None else jnp.where(live[flag] > 0, value, other)


def by_eight(x):
    return x.reshape(x.shape[0] // 8, 8, x.shape[1])


def stats_of(kv_refs, flags, factor, live, h, q, g, carried):
    top, total, dot = carried
    for kv_ref, kv_flags in zip(kv_refs, flags):
        for block, flag in enumerate(kv_flags):
            for start in range(0, kv_ref.shape[3], KEY_CHUNK_STATS):
                rows = slice(start, start + KEY_CHUNK_STATS)
                s = by_eight(contract(kv_ref[block, 0, h, rows], q, 1, 1))
                dp = by_eight(contract(kv_ref[block, 1, h, rows], g, 1, 1))
                new = jnp.maximum(top, shown(live, flag, jnp.max(s, axis=0), -jnp.inf))
                keep = jnp.exp2((top - new) * factor)
                e = jnp.exp2((s - new[None]) * factor)
                total = total * keep + shown(live, flag, jnp.sum(e, axis=0), 0.0)
                dot = dot * keep + shown(live, flag, jnp.sum(e * dp, axis=0), 0.0)
                top = new
    return top, total, dot


def stats_kernel(flags, first, factor, live, q_ref, g_ref, *refs):
    kv_refs, out_ref = refs[: len(flags)], refs[-1]
    for h in range(q_ref.shape[0]):
        if first:
            zero = jnp.zeros(out_ref.shape[2:], jnp.float32)
            carried = (jnp.full_like(zero, -jnp.inf), zero, zero)
        else:
            carried = tuple(refs[len(flags)][h, i] for i in range(3))
        result = stats_of(kv_refs, flags, factor, live, h, q_ref[h], g_ref[h], carried)
        out_ref[h, 0], out_ref[h, 1], out_ref[h, 2] = result


def grads_of(kv_refs, out_refs, flags, factor, scale, live, h, q, g, log_total, delta, acc):
    for kv_ref, out_ref, kv_flags in zip(kv_refs, out_refs, flags):
        for block, flag in enumerate(kv_flags):
            low = shown(live, flag, log_total, jnp.inf)
            k = kv_ref[block, 0, h]
            s = contract(k, q, 1, 1)
            dp = contract(kv_ref[block, 1, h], g, 1, 1)
            p = jnp.exp2(by_eight(s) * factor - low[None])
            ds = (p * (by_eight(dp) - delta[None])).reshape(s.shape).astype(jnp.bfloat16)
            dv = contract(p.reshape(s.shape).astype(jnp.bfloat16), g, 1, 0)
            dk = contract(ds, q, 1, 0) * scale
            acc = acc + contract(k, ds, 0, 0)
            out_ref[block, 0, h] = dk.astype(out_ref.dtype)
            out_ref[block, 1, h] = dv.astype(out_ref.dtype)
    return acc


def corner_kernel(flags, factor, scale, live, q_ref, g_ref, st_ref, *refs):
    count = len(flags)
    kv_refs, out_refs = refs[:count], refs[count : 2 * count]
    end_ref, acc_ref = refs[2 * count :]
    for h in range(q_ref.shape[0]):
        q, g = q_ref[h], g_ref[h]
        carried = tuple(st_ref[h, i] for i in range(3))
        top, total, dot = stats_of(kv_refs, flags, factor, live, h, q, g, carried)
        peak = jnp.max(top, axis=0, keepdims=True)
        share = jnp.exp2((top - peak) * factor)
        total = jnp.sum(share * total, axis=0, keepdims=True)
        dot = jnp.sum(share * dot, axis=0, keepdims=True)
        end_ref[h, 0] = jnp.broadcast_to(peak * factor + jnp.log2(total), top.shape)
        end_ref[h, 1] = jnp.broadcast_to(dot / total, top.shape)
        acc = jnp.zeros((q.shape[1], q.shape[0]), jnp.float32)
        acc_ref[h] = grads_of(
            kv_refs, out_refs, flags, factor, scale, live, h, q, g,
            end_ref[h, 0], end_ref[h, 1], acc,
        )


def grads_kernel(flags, last, factor, scale, live, q_ref, g_ref, end_ref, *refs):
    count = len(flags)
    kv_refs, acc_in = refs[:count], refs[count]
    out_refs, acc_ref = refs[count + 1 : 2 * count + 1], refs[2 * count + 1]
    for h in range(q_ref.shape[0]):
        acc = grads_of(
            kv_refs, out_refs, flags, factor, scale, live, h, q_ref[h], g_ref[h],
            end_ref[h, 0], end_ref[h, 1], acc_in[h],
        )
        if last:
            acc_ref[h] = (acc * scale).T.astype(jnp.bfloat16)
        else:
            acc_ref[h] = acc


def run_corner(live, q, g, stats, blocks, flags, factor, scale):
    heads, rows, depth = q.shape
    out_shape = [jax.ShapeDtypeStruct(b.shape, jnp.bfloat16) for b in blocks]
    out_shape.append(jax.ShapeDtypeStruct((heads, 2, 8, rows), jnp.float32))
    out_shape.append(jax.ShapeDtypeStruct((heads, depth, rows), jnp.float32))
    return pl.pallas_call(
        functools.partial(corner_kernel, flags, factor, scale),
        out_shape=out_shape,
        in_specs=[SMEM] + [VMEM] * (3 + len(blocks)),
        out_specs=[VMEM] * len(out_shape),
        cost_estimate=pl.CostEstimate(flops=1000, bytes_accessed=1000, transcendentals=0),
        compiler_params=pltpu.CompilerParams(vmem_limit_bytes=VMEM_LIMIT),
        name="corner",
    )(live, q, g, stats, *blocks)


def run_stats(live, q, g, blocks, flags, stats, factor, cost=1000):
    heads, rows, _ = q.shape
    first = stats is None
    args = [live, q, g, *blocks] + ([] if first else [stats])
    return pl.pallas_call(
        functools.partial(stats_kernel, flags, first, factor),
        out_shape=jax.ShapeDtypeStruct((heads, 3, 8, rows), jnp.float32),
        in_specs=[SMEM] + [VMEM] * (len(args) - 1),
        out_specs=VMEM,
        cost_estimate=pl.CostEstimate(flops=cost, bytes_accessed=1000, transcendentals=0),
        compiler_params=pltpu.CompilerParams(vmem_limit_bytes=VMEM_LIMIT),
        name="stats",
    )(*args)


def run_grads(live, q, g, ends, blocks, flags, acc, factor, scale, part, last=False):
    args = [live, q, g, ends, *blocks, acc]
    end = jax.ShapeDtypeStruct(*((q.shape, q.dtype) if last else (acc.shape, acc.dtype)))
    return pl.pallas_call(
        functools.partial(grads_kernel, flags, last, factor, scale),
        out_shape=[jax.ShapeDtypeStruct(b.shape, part) for b in blocks] + [end],
        in_specs=[SMEM] + [VMEM] * (len(args) - 1),
        out_specs=[VMEM] * (len(blocks) + 1),
        input_output_aliases={} if last else {len(args) - 1: len(blocks)},
        cost_estimate=pl.CostEstimate(flops=1000, bytes_accessed=1000, transcendentals=0),
        compiler_params=pltpu.CompilerParams(vmem_limit_bytes=VMEM_LIMIT),
        name="grads",
    )(*args)


def join_kernel(a_ref, b_ref, out_ref):
    out_ref[0] = a_ref[0]
    out_ref[1] = b_ref[0]


def run_join(a, b):
    return pl.pallas_call(
        join_kernel,
        out_shape=jax.ShapeDtypeStruct((2,) + a.shape[1:], a.dtype),
        in_specs=[VMEM] * 2,
        out_specs=VMEM,
        cost_estimate=pl.CostEstimate(flops=1000, bytes_accessed=1000, transcendentals=0),
        compiler_params=pltpu.CompilerParams(vmem_limit_bytes=VMEM_LIMIT),
        name="join",
    )(a, b)


def relay_kernel(own_a, own_b, from_a, from_b, out_a, out_b):
    for block, (own, out) in enumerate(((own_a, out_a), (own_b, out_b))):
        out[0] = (
            own[0]
            + from_a[block].astype(jnp.float32)
            + from_b[block].astype(jnp.float32)
        ).astype(out.dtype)


def run_relay(own_a, own_b, from_a, from_b):
    return pl.pallas_call(
        relay_kernel,
        out_shape=[jax.ShapeDtypeStruct(own_a.shape, jnp.bfloat16)] * 2,
        in_specs=[VMEM] * 4,
        out_specs=[VMEM] * 2,
        cost_estimate=pl.CostEstimate(flops=1000, bytes_accessed=1000, transcendentals=0),
        compiler_params=pltpu.CompilerParams(vmem_limit_bytes=VMEM_LIMIT),
        name="relay",
    )(own_a, own_b, from_a, from_b)


def total_kernel(own, *refs):
    parts, outs = refs[:-2], refs[-2:]
    for which, out in enumerate(outs):
        total = own[0, which]
        for part in parts:
            total = total + part[0, which].astype(jnp.float32)
        out[...] = total.astype(out.dtype)


def run_total(own, parts):
    return pl.pallas_call(
        total_kernel,
        out_shape=[jax.ShapeDtypeStruct(own.shape[2:], jnp.bfloat16)] * 2,
        in_specs=[VMEM] * (1 + len(parts)),
        out_specs=[VMEM] * 2,
        cost_estimate=pl.CostEstimate(flops=1000, bytes_accessed=1000, transcendentals=0),
        compiler_params=pltpu.CompilerParams(vmem_limit_bytes=VMEM_LIMIT),
        name="total",
    )(own, *parts)


def partner(at, pair):
    odd = at % 2
    return at + (1 - 2 * odd) * (1 - 2 * pair)


def swapped(x, stage, pair, sizes):
    frames, rows, heads = sizes
    route = []
    for f in range(frames):
        for r in range(rows):
            for h in range(heads):
                along_rows = (h + stage) % 2
                to_f = f if along_rows else partner(f, pair)
                to_r = partner(r, pair) if along_rows else r
                if 0 <= to_f < frames and 0 <= to_r < rows:
                    route.append(
                        ((f * rows + r) * heads + h, (to_f * rows + to_r) * heads + h)
                    )
    return lax.ppermute(x, ("tm", "height", "head"), route)


def local(query_in, key_in, value_in, out_grad):
    shape = query_in.shape
    heads, depth = shape[0], shape[-1]
    flat = (heads, math.prod(shape[1:4]), depth)
    scale = depth**-0.5
    factor = scale * math.log2(math.e)
    q, g = query_in.reshape(flat), out_grad.reshape(flat)
    kv = jnp.stack([key_in.reshape(flat), value_in.reshape(flat)])[None]
    sizes = tuple(lax.axis_size(a) for a in ("tm", "height", "head"))
    frame, row = lax.axis_index("tm"), lax.axis_index("height")
    frames_first = lax.axis_index("head") % 2 == 0
    place = (jnp.where(frames_first, frame, row), jnp.where(frames_first, row, frame))
    size = (
        jnp.where(frames_first, sizes[0], sizes[1]),
        jnp.where(frames_first, sizes[1], sizes[0]),
    )
    met = [[partner(place[i], pair) for pair in (0, 1)] for i in (0, 1)]
    first, second = [
        [((m >= 0) & (m < size[i])).astype(jnp.int32) for m in met[i]] for i in (0, 1)
    ]
    live = jnp.stack(first + second + [b * a for b in second for a in first])

    first_a, first_b = (swapped(kv, 0, pair, sizes) for pair in (0, 1))
    stats = run_stats(live, q, g, [kv], [[None]], None, factor)
    later, stats, first_a = lax.optimization_barrier((kv, stats, first_a))
    second_a, second_b = (swapped(later, 1, pair, sizes) for pair in (0, 1))
    both = run_join(first_a, first_b)
    corner_b, corner_a = (swapped(both, 1, pair, sizes) for pair in (1, 0))

    near, near_flags = [first_a, first_b, kv], [[0], [1], [None]]
    side, side_flags = [second_a, second_b], [[2], [3]]
    corner, corner_flags = [corner_b, corner_a], [[6, 7], [4, 5]]
    stats = run_stats(live, q, g, near[:2], near_flags[:2], stats, factor)
    stats = run_stats(live, q, g, side, side_flags, stats, factor, cost=20 * 10**12)
    part_b, part_a, ends, acc = run_corner(
        live, q, g, stats, corner, corner_flags, factor, scale
    )
    back_b = swapped(part_b, 1, 1, sizes)
    back_a = swapped(part_a, 1, 0, sizes)
    grads = functools.partial(run_grads, live, q, g, ends)
    side_a, side_b, acc = grads(side, side_flags, acc, factor, scale, jnp.bfloat16)
    from_b = swapped(side_b, 1, 1, sizes)
    total_parts = [from_b, swapped(side_a, 1, 0, sizes)]
    own_a, own_b, own, dq = grads(near, near_flags, acc, factor, scale, jnp.float32, last=True)
    send_a, send_b = run_relay(own_a, own_b, back_b, back_a)
    got_b = swapped(send_b, 0, 1, sizes)
    total_parts += [got_b, swapped(send_a, 0, 0, sizes)]
    dk, dv = run_total(own, total_parts)
    return dq.reshape(shape), dk.reshape(shape), dv.reshape(shape)


def solution(mesh):
    spec = P("head", "tm", "height", None, None)
    return jax.shard_map(
        local, mesh=mesh, in_specs=(spec,) * 4, out_specs=(spec,) * 3, check_vma=False
    )
```

```python
import functools
import math

import jax
import jax.numpy as jnp
from jax import lax
from jax.experimental import pallas as pl
from jax.experimental.pallas import tpu as pltpu
from jax.sharding import PartitionSpec as P

KEY_CHUNK_STATS = 128
VMEM_LIMIT = 16 << 20
VMEM = pl.BlockSpec(memory_space=pltpu.VMEM)
SMEM = pl.BlockSpec(memory_space=pltpu.SMEM)


def contract(a, b, dim_a, dim_b):
    return lax.dot_general(
        a, b, (((dim_a,), (dim_b,)), ((), ())), preferred_element_type=jnp.float32
    )


def shown(live, flag, value, other):
    return value if flag is None else jnp.where(live[flag] > 0, value, other)


def by_eight(x):
    return x.reshape(x.shape[0] // 8, 8, x.shape[1])


def stats_of(kv_refs, flags, factor, live, h, q, g, carried):
    top, total, dot = carried
    for kv_ref, kv_flags in zip(kv_refs, flags):
        for block, flag in enumerate(kv_flags):
            for start in range(0, kv_ref.shape[3], KEY_CHUNK_STATS):
                rows = slice(start, start + KEY_CHUNK_STATS)
                s = by_eight(contract(kv_ref[block, 0, h, rows], q, 1, 1))
                dp = by_eight(contract(kv_ref[block, 1, h, rows], g, 1, 1))
                new = jnp.maximum(top, shown(live, flag, jnp.max(s, axis=0), -jnp.inf))
                keep = jnp.exp2((top - new) * factor)
                e = jnp.exp2((s - new[None]) * factor)
                total = total * keep + shown(live, flag, jnp.sum(e, axis=0), 0.0)
                dot = dot * keep + shown(live, flag, jnp.sum(e * dp, axis=0), 0.0)
                top = new
    return top, total, dot


def stats_kernel(flags, first, factor, live, q_ref, g_ref, *refs):
    kv_refs, out_ref = refs[: len(flags)], refs[-1]
    for h in range(q_ref.shape[0]):
        if first:
            zero = jnp.zeros(out_ref.shape[2:], jnp.float32)
            carried = (jnp.full_like(zero, -jnp.inf), zero, zero)
        else:
            carried = tuple(refs[len(flags)][h, i] for i in range(3))
        result = stats_of(kv_refs, flags, factor, live, h, q_ref[h], g_ref[h], carried)
        out_ref[h, 0], out_ref[h, 1], out_ref[h, 2] = result


def grads_of(kv_refs, out_refs, flags, factor, scale, live, h, q, g, log_total, delta, acc):
    for kv_ref, out_ref, kv_flags in zip(kv_refs, out_refs, flags):
        for block, flag in enumerate(kv_flags):
            low = shown(live, flag, log_total, jnp.inf)
            k = kv_ref[block, 0, h]
            s = contract(k, q, 1, 1)
            dp = contract(kv_ref[block, 1, h], g, 1, 1)
            p = jnp.exp2(by_eight(s) * factor - low[None])
            ds = (p * (by_eight(dp) - delta[None])).reshape(s.shape).astype(jnp.bfloat16)
            dv = contract(p.reshape(s.shape).astype(jnp.bfloat16), g, 1, 0)
            dk = contract(ds, q, 1, 0) * scale
            acc = acc + contract(k, ds, 0, 0)
            out_ref[block, 0, h] = dk.astype(out_ref.dtype)
            out_ref[block, 1, h] = dv.astype(out_ref.dtype)
    return acc


def corner_kernel(flags, factor, scale, live, q_ref, g_ref, st_ref, *refs):
    count = len(flags)
    kv_refs, out_refs = refs[:count], refs[count : 2 * count]
    end_ref, acc_ref = refs[2 * count :]
    for h in range(q_ref.shape[0]):
        q, g = q_ref[h], g_ref[h]
        carried = tuple(st_ref[h, i] for i in range(3))
        top, total, dot = stats_of(kv_refs, flags, factor, live, h, q, g, carried)
        peak = jnp.max(top, axis=0, keepdims=True)
        share = jnp.exp2((top - peak) * factor)
        total = jnp.sum(share * total, axis=0, keepdims=True)
        dot = jnp.sum(share * dot, axis=0, keepdims=True)
        end_ref[h, 0] = jnp.broadcast_to(peak * factor + jnp.log2(total), top.shape)
        end_ref[h, 1] = jnp.broadcast_to(dot / total, top.shape)
        acc = jnp.zeros((q.shape[1], q.shape[0]), jnp.float32)
        acc_ref[h] = grads_of(
            kv_refs, out_refs, flags, factor, scale, live, h, q, g,
            end_ref[h, 0], end_ref[h, 1], acc,
        )


def grads_kernel(flags, last, factor, scale, live, q_ref, g_ref, end_ref, *refs):
    count = len(flags)
    kv_refs, acc_in = refs[:count], refs[count]
    out_refs, acc_ref = refs[count + 1 : 2 * count + 1], refs[2 * count + 1]
    for h in range(q_ref.shape[0]):
        acc = grads_of(
            kv_refs, out_refs, flags, factor, scale, live, h, q_ref[h], g_ref[h],
            end_ref[h, 0], end_ref[h, 1], acc_in[h],
        )
        if last:
            acc_ref[h] = (acc * scale).T.astype(jnp.bfloat16)
        else:
            acc_ref[h] = acc


def run_corner(live, q, g, stats, blocks, flags, factor, scale):
    heads, rows, depth = q.shape
    out_shape = [jax.ShapeDtypeStruct(b.shape, jnp.bfloat16) for b in blocks]
    out_shape.append(jax.ShapeDtypeStruct((heads, 2, 8, rows), jnp.float32))
    out_shape.append(jax.ShapeDtypeStruct((heads, depth, rows), jnp.float32))
    return pl.pallas_call(
        functools.partial(corner_kernel, flags, factor, scale),
        out_shape=out_shape,
        in_specs=[SMEM] + [VMEM] * (3 + len(blocks)),
        out_specs=[VMEM] * len(out_shape),
        cost_estimate=pl.CostEstimate(flops=1000, bytes_accessed=1000, transcendentals=0),
        compiler_params=pltpu.CompilerParams(vmem_limit_bytes=VMEM_LIMIT),
        name="corner",
    )(live, q, g, stats, *blocks)


def run_stats(live, q, g, blocks, flags, stats, factor, cost=1000):
    heads, rows, _ = q.shape
    first = stats is None
    args = [live, q, g, *blocks] + ([] if first else [stats])
    return pl.pallas_call(
        functools.partial(stats_kernel, flags, first, factor),
        out_shape=jax.ShapeDtypeStruct((heads, 3, 8, rows), jnp.float32),
        in_specs=[SMEM] + [VMEM] * (len(args) - 1),
        out_specs=VMEM,
        cost_estimate=pl.CostEstimate(flops=cost, bytes_accessed=1000, transcendentals=0),
        compiler_params=pltpu.CompilerParams(vmem_limit_bytes=VMEM_LIMIT),
        name="stats",
    )(*args)


def run_grads(live, q, g, ends, blocks, flags, acc, factor, scale, types, last=False):
    args = [live, q, g, ends, *blocks, acc]
    end = jax.ShapeDtypeStruct(*((q.shape, q.dtype) if last else (acc.shape, acc.dtype)))
    return pl.pallas_call(
        functools.partial(grads_kernel, flags, last, factor, scale),
        out_shape=[jax.ShapeDtypeStruct(b.shape, t) for b, t in zip(blocks, types)] + [end],
        in_specs=[SMEM] + [VMEM] * (len(args) - 1),
        out_specs=[VMEM] * (len(blocks) + 1),
        input_output_aliases={} if last else {len(args) - 1: len(blocks)},
        cost_estimate=pl.CostEstimate(flops=1000, bytes_accessed=1000, transcendentals=0),
        compiler_params=pltpu.CompilerParams(vmem_limit_bytes=VMEM_LIMIT),
        name="grads",
    )(*args)


def join_kernel(a_ref, b_ref, out_ref):
    out_ref[0] = a_ref[0]
    out_ref[1] = b_ref[0]


def run_join(a, b):
    return pl.pallas_call(
        join_kernel,
        out_shape=jax.ShapeDtypeStruct((2,) + a.shape[1:], a.dtype),
        in_specs=[VMEM] * 2,
        out_specs=VMEM,
        cost_estimate=pl.CostEstimate(flops=1000, bytes_accessed=1000, transcendentals=0),
        compiler_params=pltpu.CompilerParams(vmem_limit_bytes=VMEM_LIMIT),
        name="join",
    )(a, b)


def relay_kernel(own_a, own_b, from_a, from_b, out_a, out_b):
    for block, (own, out) in enumerate(((own_a, out_a), (own_b, out_b))):
        out[0] = (
            own[0]
            + from_a[block].astype(jnp.float32)
            + from_b[block].astype(jnp.float32)
        ).astype(out.dtype)


def run_relay(own_a, own_b, from_a, from_b):
    return pl.pallas_call(
        relay_kernel,
        out_shape=[jax.ShapeDtypeStruct(own_a.shape, jnp.bfloat16)] * 2,
        in_specs=[VMEM] * 4,
        out_specs=[VMEM] * 2,
        cost_estimate=pl.CostEstimate(flops=1000, bytes_accessed=1000, transcendentals=0),
        compiler_params=pltpu.CompilerParams(vmem_limit_bytes=VMEM_LIMIT),
        name="relay",
    )(own_a, own_b, from_a, from_b)


def total_kernel(own, *refs):
    parts, outs = refs[:-2], refs[-2:]
    for which, out in enumerate(outs):
        total = own[0, which]
        for part in parts:
            total = total + part[0, which].astype(jnp.float32)
        out[...] = total.astype(out.dtype)


def run_total(own, parts):
    return pl.pallas_call(
        total_kernel,
        out_shape=[jax.ShapeDtypeStruct(own.shape[2:], jnp.bfloat16)] * 2,
        in_specs=[VMEM] * (1 + len(parts)),
        out_specs=[VMEM] * 2,
        cost_estimate=pl.CostEstimate(flops=1000, bytes_accessed=1000, transcendentals=0),
        compiler_params=pltpu.CompilerParams(vmem_limit_bytes=VMEM_LIMIT),
        name="total",
    )(own, *parts)


def partner(at, pair):
    odd = at % 2
    return at + (1 - 2 * odd) * (1 - 2 * pair)


def swapped(x, stage, pair, sizes):
    frames, rows, heads = sizes
    route = []
    for f in range(frames):
        for r in range(rows):
            for h in range(heads):
                along_rows = (h + stage) % 2
                to_f = f if along_rows else partner(f, pair)
                to_r = partner(r, pair) if along_rows else r
                if 0 <= to_f < frames and 0 <= to_r < rows:
                    route.append(
                        ((f * rows + r) * heads + h, (to_f * rows + to_r) * heads + h)
                    )
    return lax.ppermute(x, ("tm", "height", "head"), route)


def local(query_in, key_in, value_in, out_grad):
    shape = query_in.shape
    heads, depth = shape[0], shape[-1]
    flat = (heads, math.prod(shape[1:4]), depth)
    scale = depth**-0.5
    factor = scale * math.log2(math.e)
    q, g = query_in.reshape(flat), out_grad.reshape(flat)
    kv = jnp.stack([key_in.reshape(flat), value_in.reshape(flat)])[None]
    sizes = tuple(lax.axis_size(a) for a in ("tm", "height", "head"))
    frame, row = lax.axis_index("tm"), lax.axis_index("height")
    frames_first = lax.axis_index("head") % 2 == 0
    place = (jnp.where(frames_first, frame, row), jnp.where(frames_first, row, frame))
    size = (
        jnp.where(frames_first, sizes[0], sizes[1]),
        jnp.where(frames_first, sizes[1], sizes[0]),
    )
    met = [[partner(place[i], pair) for pair in (0, 1)] for i in (0, 1)]
    first, second = [
        [((m >= 0) & (m < size[i])).astype(jnp.int32) for m in met[i]] for i in (0, 1)
    ]
    live = jnp.stack(first + second + [b * a for b in second for a in first])

    first_a, first_b = (swapped(kv, 0, pair, sizes) for pair in (0, 1))
    stats = run_stats(live, q, g, [kv], [[None]], None, factor)
    later, stats, first_a = lax.optimization_barrier((kv, stats, first_a))
    second_a, second_b = (swapped(later, 1, pair, sizes) for pair in (0, 1))
    both = run_join(first_a, first_b)
    corner_b, corner_a = (swapped(both, 1, pair, sizes) for pair in (1, 0))

    near, near_flags = [first_a, first_b, kv], [[0], [1], [None]]
    side, side_flags = [second_a, second_b], [[2], [3]]
    corner, corner_flags = [corner_b, corner_a], [[6, 7], [4, 5]]
    stats = run_stats(live, q, g, near[:2], near_flags[:2], stats, factor)
    stats = run_stats(live, q, g, side, side_flags, stats, factor, cost=20 * 10**12)
    part_b, part_a, ends, acc = run_corner(
        live, q, g, stats, corner, corner_flags, factor, scale
    )
    back_b = swapped(part_b, 1, 1, sizes)
    back_a = swapped(part_a, 1, 0, sizes)
    types = [jnp.bfloat16] * 2 + [jnp.float32] * 3
    side_a, side_b, own_a, own_b, own, dq = run_grads(
        live, q, g, ends, side + near, side_flags + near_flags, acc, factor, scale, types, last=True
    )
    from_b = swapped(side_b, 1, 1, sizes)
    total_parts = [from_b, swapped(side_a, 1, 0, sizes)]
    send_a, send_b = run_relay(own_a, own_b, back_b, back_a)
    got_b = swapped(send_b, 0, 1, sizes)
    total_parts += [got_b, swapped(send_a, 0, 0, sizes)]
    dk, dv = run_total(own, total_parts)
    return dq.reshape(shape), dk.reshape(shape), dv.reshape(shape)


def solution(mesh):
    spec = P("head", "tm", "height", None, None)
    return jax.shard_map(
        local, mesh=mesh, in_specs=(spec,) * 4, out_specs=(spec,) * 3, check_vma=False
    )
```
